256 devices in a mesh: leaf: 256 (over x, z, y, core).
Axes of the slice: x: 4, y: 4, z: 8, core: 2. Of those that a mesh axis runs over, the one named last changes fastest.
Arguments:
- points: bfloat16 [64, 1048576], P(None, 'leaf'), may hold values from -5 to 5
- charges: bfloat16 [32, 1048576], P(None, 'leaf'), may hold values from -1.5 to 1.5
- leaf_order: int32 [256, 4096], P('leaf'), may hold values from 0 to 4095, each once within a row
- near_list: int32 [4096, 16], P('leaf'), may hold values from -1 to 4095, as said below
- far_list: int32 [2048, 8], P('leaf'), may hold values from -1 to 7
- local_skel: int32 [3840, 256], P('leaf'), may hold values from 0 to 511, as said below
- upper_skel: int32 [254, 256], replicated, may hold values from 0 to 511, as said below
Outputs:
- potentials: float32 [32, 1048576], P(None, 'leaf')
- root_field: float32 [256, 32, 256], P('leaf')
The draws below stay inside these ranges and needn't reach their ends.
Inputs may be any that keep to these rules, and one draw needn't show every extreme that they name: `leaf_order`: each row is a permutation of the positions of one device's points. `near_list`: slot 0 of leaf g's row is g itself; every other entry is -1 or a leaf h different from g with |h - g| <= 16, and the leaves of one row are distinct. `far_list`: an entry other than -1 names a level-one node of the same device subtree, counted from that subtree's first level-one node; entries of a row may repeat. `local_skel`: the entries of a row are distinct. `upper_skel`: the entries of a row are distinct.
All inputs are finite; a program needn't handle non-finite values.
Results may differ from the reference program's by a relative error of at most 0.0014.
Values may be sent and summed in bfloat16 or wider, within the bound.
A program may use at most 64 MiB of HBM per device.

```python
import math
import jax
import jax.numpy as jnp
from jax import lax

FEAT = 64
LEAF_PTS = 256
SKEL = 256
RHS = 32
NEAR = 16
FAR = 8
LEAF_DEV = 16
LOCAL_LEV = 4
UPPER = 8
PTS_DEV = 4096
LEAVES = 4096
POINTS = 1048576
N_LEAF = 256


def distinct_rows(key, row_count, pool_size, count_taken):
    scores = jax.random.randint(key, (row_count, pool_size), 0, 1 << 20) * pool_size
    scores = scores + jnp.arange(pool_size, dtype=jnp.int32)[None, :]
    return jnp.argsort(scores, axis=1)[:, :count_taken].astype(jnp.int32)


def draw_near_list(key, part):
    leaf_total = N_LEAF * LEAF_DEV
    picks = distinct_rows(jax.random.fold_in(key, 7), leaf_total, 2 * LEAF_DEV, NEAR - 1)
    offsets = jnp.where(picks < LEAF_DEV, picks - LEAF_DEV, picks - LEAF_DEV + 1)
    self_ids = jnp.arange(leaf_total, dtype=jnp.int32)[:, None]
    others = self_ids + offsets
    dropped = jax.random.randint(jax.random.fold_in(key, 8), (leaf_total, NEAR - 1), 0, 8) == 0
    others = jnp.where((others < 0) | (others >= leaf_total) | dropped, -1, others)
    others = others.at[0, NEAR - 2].set(-1)
    return jnp.concatenate([self_ids, others], axis=1).astype(jnp.int32)


def draw_local_skel(key, part):
    return distinct_rows(jax.random.fold_in(key, 11), N_LEAF * (LEAF_DEV - 1), 2 * SKEL, SKEL)


def draw_upper_skel(key, part):
    return distinct_rows(jax.random.fold_in(key, 13), N_LEAF - 2, 2 * SKEL, SKEL)


def touch_ends(drawn, rng, low, largest):
    place = [jax.random.randint(jax.random.fold_in(rng, axis), (), 0, length) for axis, length in enumerate(drawn.shape)]
    main_axis = drawn.shape.index(max(drawn.shape))
    neighbour = place[:main_axis] + [(place[main_axis] + 1) % drawn.shape[main_axis]] + place[main_axis + 1:]
    return drawn.at[tuple(place)].set(low).at[tuple(neighbour)].set(largest)


def shard_levels(own_key, shape, pieces, smallest, top_value):
    def one(axis_at, shards_of):
        draws = jax.random.uniform(jax.random.fold_in(jax.random.fold_in(own_key, 6), axis_at), (shards_of,), jnp.float32, smallest / len(pieces), top_value / len(pieces))
        return jnp.repeat(jnp.exp(draws), shape[axis_at] // shards_of).reshape((-1,) + (1,) * (len(shape) - axis_at - 1))

    factor_of = one(*pieces[0])
    for cut in pieces[1:]:
        factor_of = factor_of * one(*cut)
    return factor_of


def normal_values(stream_key, dims, scale, limit, split=(), held_as=jnp.bfloat16):
    values = jax.random.normal(stream_key, dims, jnp.float32) * scale
    if len(split) > 0:
        values = shard_levels(stream_key, dims, split, -0.22, 0.18) * values
    return jnp.clip(values, min=-limit, max=limit).astype(held_as)


def setup_inputs(seed: int = 0) -> dict:
    splits = jax.random.split(jax.random.key(seed), 8)
    return {
        "points": normal_values(splits[0], (FEAT, POINTS), 1.0, 5.0, ((1, 256),)),
        "charges": normal_values(splits[1], (RHS, POINTS), 0.25, 1.5, ((1, 256),)),
        "leaf_order": jax.vmap(lambda own: jax.random.permutation(own, PTS_DEV))(jax.random.split(splits[2], N_LEAF)).reshape((N_LEAF, PTS_DEV)).astype(jnp.int32),
        "near_list": draw_near_list(jax.random.fold_in(splits[7], 71), 0),
        "far_list": touch_ends(jax.random.randint(splits[4], (LEAVES // 2, FAR), -1, LEAF_DEV // 2), jax.random.fold_in(splits[4], 1), -1, (LEAF_DEV // 2) - 1).astype(jnp.int32),
        "local_skel": draw_local_skel(jax.random.fold_in(splits[7], 71), 0),
        "upper_skel": draw_upper_skel(jax.random.fold_in(splits[7], 71), 0),
    }


pair_gain = math.sqrt(2.0)

def matern(source, target, kern_scale):
    inner_prod = lax.dot_general(source, target, (((0,), (0,)), ((), ())), preferred_element_type=jnp.float32)
    source_sq = lax.optimization_barrier(jnp.sum(jnp.square(source.astype(jnp.float32)), axis=0))
    target_sq = lax.optimization_barrier(jnp.sum(jnp.square(target.astype(jnp.float32)), axis=0))
    spread = jnp.maximum(source_sq[:, None] + target_sq[None, :] - 2.0 * inner_prod, 0.0)
    radius = jnp.sqrt(spread) * kern_scale
    return ((1.0 + radius) * jnp.exp(-radius)).astype(jnp.bfloat16)

def transfer(source, target, weights, kern_scale):
    return jnp.dot(weights, matern(source, target, kern_scale), preferred_element_type=jnp.float32)

def averaged(source, target, weights, kern_scale):
    kernel = matern(source, target, kern_scale)
    column_total = lax.optimization_barrier(jnp.sum(kernel.astype(jnp.float32), axis=0))
    return jnp.dot(weights, kernel, preferred_element_type=jnp.float32) / column_total[None, :]

def join_halves(stacked):
    node_count, row_count, col_count = stacked.shape
    paired = stacked.reshape(node_count // 2, 2, row_count, col_count).transpose(0, 2, 1, 3)
    return paired.reshape(node_count // 2, row_count, 2 * col_count)

def split_halves(joined):
    node_count, row_count, col_count = joined.shape
    halves = joined.reshape(node_count, row_count, 2, col_count // 2).transpose(0, 2, 1, 3)
    return halves.reshape(2 * node_count, row_count, col_count // 2)

def reference(points, charges, leaf_order, near_list, far_list, local_skel, upper_skel):
    kern_scale = 2.0 * math.sqrt(3.0 / FEAT)
    leaf_total = N_LEAF * LEAF_DEV
    top_height = LOCAL_LEV + UPPER
    tree_order = (leaf_order + (jnp.arange(N_LEAF, dtype=jnp.int32) * PTS_DEV)[:, None]).reshape(-1)
    leaf_points = jnp.take(points, tree_order, axis=1).reshape(FEAT, leaf_total, LEAF_PTS).transpose(1, 0, 2)
    leaf_charges = jnp.take(charges, tree_order, axis=1).reshape(RHS, leaf_total, LEAF_PTS).transpose(1, 0, 2)

    def near_one(bundle):
        target, slot_ids = bundle

        def add_slot(running, slot_id):
            safe_id = jnp.maximum(slot_id, 0)
            contribution = transfer(leaf_points[safe_id], target, leaf_charges[safe_id], kern_scale)
            return (running + contribution * (slot_id >= 0).astype(jnp.float32), None)
        row_total, _ = lax.scan(add_slot, jnp.zeros((RHS, LEAF_PTS), jnp.float32), slot_ids)
        return row_total
    near_field = lax.map(near_one, (leaf_points, near_list))

    def lift_node(bundle):
        return (pair_gain * averaged(bundle[0], bundle[1], bundle[2], kern_scale)).astype(jnp.bfloat16)

    def couple_node(bundle):
        return transfer(bundle[0], bundle[1], bundle[2], kern_scale)

    def push_node(bundle):
        return averaged(bundle[0], bundle[1], bundle[2].astype(jnp.bfloat16), kern_scale)
    node_points = [leaf_points]
    node_weights = [leaf_charges]
    joined_points = [None]
    for height in range(1, top_height):
        pair_points = join_halves(node_points[-1])
        pair_weights = join_halves(node_weights[-1])
        node_count = leaf_total >> height
        node_ids = jnp.arange(node_count, dtype=jnp.int32)
        if height <= LOCAL_LEV:
            per_device = LEAF_DEV >> height
            table_rows = node_ids // per_device * (LEAF_DEV - 1) + (LEAF_DEV - (LEAF_DEV >> height - 1)) + node_ids % per_device
            chosen = local_skel[table_rows]
        else:
            table_rows = N_LEAF - (N_LEAF >> height - LOCAL_LEV - 1) + node_ids
            chosen = upper_skel[table_rows]
        parent_points = jnp.take_along_axis(pair_points, chosen[:, None, :], axis=2)
        parent_weights = lax.map(lift_node, (pair_points, parent_points, pair_weights))
        node_points.append(parent_points)
        node_weights.append(parent_weights)
        joined_points.append(pair_points)
    fields = [None] * top_height
    for height in range(1, top_height):
        here_points = node_points[height]
        here_weights = node_weights[height]
        partner = jnp.arange(here_points.shape[0], dtype=jnp.int32) ^ 1
        coupled = lax.map(couple_node, (here_points[partner], here_points, here_weights[partner]))
        if height == 1:
            per_node = LEAF_DEV // 2
            base_ids = jnp.arange(leaf_total // 2, dtype=jnp.int32) // per_node * per_node

            def far_one(bundle):
                target, entries, base_id = bundle

                def add_entry(running, entry):
                    safe_id = base_id + jnp.maximum(entry, 0)
                    contribution = transfer(here_points[safe_id], target, here_weights[safe_id], kern_scale)
                    return (running + contribution * (entry >= 0).astype(jnp.float32), None)
                row_total, _ = lax.scan(add_entry, jnp.zeros((RHS, SKEL), jnp.float32), entries)
                return row_total
            coupled = coupled + lax.map(far_one, (here_points, far_list, base_ids))
        fields[height] = coupled
    leaf_field = None
    root_field = None
    for height in range(top_height - 1, 0, -1):
        if height == LOCAL_LEV:
            root_field = fields[height]
        pushed = lax.map(push_node, (node_points[height], joined_points[height], fields[height]))
        spread = split_halves(pushed)
        if height > 1:
            fields[height - 1] = fields[height - 1] + spread
        else:
            leaf_field = spread
    tree_rows = (leaf_field + near_field).transpose(1, 0, 2).reshape(RHS, POINTS)
    potentials = jnp.zeros((RHS, POINTS), jnp.float32).at[:, tree_order].set(tree_rows)
    return (potentials, root_field)
```

```python
import functools
import math

import jax
import jax.numpy as jnp
from jax import lax
from jax.experimental import pallas as pl
from jax.experimental.pallas import tpu as pltpu
from jax.sharding import PartitionSpec as P

f32 = jnp.float32
bf16 = jnp.bfloat16
MESH = pl.DeviceIdType.MESH
gain = math.sqrt(2.0)

LEFT, OWN, NODE, ZERO, RIGHT = 0, 16, 32, 47, 48


def dot(a, b):
    return jnp.dot(a, b, preferred_element_type=f32)


def dot_t(a, b):
    return lax.dot_general(a, b, (((1,), (1,)), ((), ())), preferred_element_type=f32)


def matern(scale, dist):
    positive = jnp.maximum(dist, 1e-30)
    radius = positive * lax.rsqrt(positive)
    return ((1.0 + radius * scale) * jnp.exp2(radius * (-scale * math.log2(math.e)))).astype(bf16)


def rows_of(block):
    columns = jnp.concatenate(
        [
            block[0:64].astype(f32) * -0.5,
            jnp.zeros((32, block.shape[1]), f32),
            block[112:128].astype(f32),
            block[96:112].astype(f32),
        ],
        axis=0,
    )
    return columns.T.astype(bf16)


def block_of(stacked):
    coords = stacked[0:64]
    square = jnp.sum(coords * coords, axis=0, keepdims=True)
    high = square.astype(bf16).astype(f32)
    rest = square - high
    middle = rest.astype(bf16).astype(f32)
    low = rest - middle
    place = lax.broadcasted_iota(jnp.int32, (16, stacked.shape[1]), 0)
    ones = jnp.where(place < 3, 1.0, 0.0)
    terms = jnp.where(place == 0, high, jnp.where(place == 1, middle, jnp.where(place == 2, low, 0.0)))
    return jnp.concatenate([coords * -2.0, stacked[64:96], ones, terms], axis=0).astype(bf16)


def one_hot(chosen, first, height=256):
    place = lax.broadcasted_iota(jnp.int32, (height, chosen.shape[1]), 0)
    return jnp.where(place == chosen - first, 1.0, 0.0).astype(bf16)


def lift(scale, left_block, right_block, left_rows, right_rows, chosen, kernel_ref):
    picked = dot(left_block, one_hot(chosen, 0)) + dot(right_block, one_hot(chosen, 256))
    target = picked.astype(bf16)
    first = matern(scale, dot(left_rows, target))
    second = matern(scale, dot(right_rows, target))
    kernel_ref[0] = first
    kernel_ref[1] = second
    sums = dot(left_block[64:112], first) + dot(right_block[64:112], second)
    weights = (gain * (sums[0:32] / sums[32:33])).astype(bf16)
    block = jnp.concatenate([target[0:64], weights, target[96:128]], axis=0)
    return block, rows_of(block)


def pushed(field, kernel):
    high = jnp.concatenate([field.astype(bf16), jnp.ones((16, field.shape[1]), bf16)], axis=0)
    sums = dot_t(high, kernel)
    return sums[0:32] / sums[32:33]


def sort_in(points, charges, order, source, blocks, rows):
    def fill(b, _):
        lanes = pl.ds(pl.multiple_of(b * 256, 256), 256)
        source[b, 0:64] = points[:, lanes]
        source[b, 64:96] = charges[:, lanes]
        return 0

    lax.fori_loop(0, 16, fill, 0)

    def leaf(g, _):
        ids = order[:, pl.ds(pl.multiple_of(g * 256, 256), 256)]
        found = dot(source[...].reshape(16 * 96, 256), one_hot(ids & 255, 0))
        high = ids >> 8
        stacked = found[0:96]
        for b in range(1, 16):
            stacked = jnp.where(high == b, found[b * 96 : b * 96 + 96], stacked)
        block = block_of(stacked)
        blocks[OWN + g] = block
        rows[OWN + g] = rows_of(block)
        return 0

    lax.fori_loop(0, 16, leaf, 0)


def sort_out(order, fields, output):
    output[...] = jnp.zeros_like(output)

    def leaf(g, _):
        ids = order[:, pl.ds(pl.multiple_of(g * 256, 256), 256)]
        picks = one_hot(ids & 255, 0)
        high = ids >> 8
        value = fields[g]
        first = value.astype(bf16).astype(f32)
        rest = value - first
        second = rest.astype(bf16).astype(f32)
        third = rest - second
        terms = jnp.concatenate([first, second, third], axis=0)
        for part in range(4):
            masked = jnp.concatenate(
                [jnp.where(high == part * 4 + b, terms, 0.0).astype(bf16) for b in range(4)], axis=0
            )
            found = dot_t(masked, picks)
            for b in range(4):
                lanes = slice((part * 4 + b) * 256, (part * 4 + b + 1) * 256)
                piece = found[b * 96 : b * 96 + 96]
                output[:, lanes] += piece[0:32] + piece[32:64] + piece[64:96]
        return 0

    lax.fori_loop(0, 16, leaf, 0)


def local_up(scale, skel, blocks, rows, kernels):
    def one(n):
        a, b = OWN + 2 * n, OWN + 1 + 2 * n
        block, flat = lift(
            scale, blocks[a], blocks[b], rows[a], rows[b], skel[pl.ds(n, 1), :], kernels.at[n]
        )
        blocks[NODE + n] = block
        rows[NODE + n] = flat

    def two(p, _):
        one(2 * p)
        one(2 * p + 1)
        return 0

    lax.fori_loop(0, 7, two, 0)
    one(14)


def local_down(fields, kernels):
    def one(n):
        field = fields[16 + n]
        fields[2 * n] += pushed(field, kernels[n, 0])
        fields[2 * n + 1] += pushed(field, kernels[n, 1])

    one(14)

    def two(p, _):
        one(13 - 2 * p)
        one(12 - 2 * p)
        return 0

    lax.fori_loop(0, 7, two, 0)


def couple_pair(scale, blocks, rows, fields, a, b):
    kernel = matern(scale, dot(rows[NODE + a], blocks[NODE + b]))
    fields[16 + b] = dot(blocks[NODE + a, 64:96], kernel)
    fields[16 + a] = dot_t(blocks[NODE + b, 64:96], kernel)


def far_counts(far_list):
    def count(i, b):
        total = jnp.where(b == i + 1 - 2 * (i % 2), 1.0, 0.0)
        for e in range(8):
            total = total + jnp.where(far_list[i, e] == b, 1.0, 0.0)
        return total

    return count


def far_own(scale, count, blocks, rows, fields):
    def own(i, _):
        kernel = matern(scale, dot(rows[NODE + i], blocks[NODE + i]))
        fields[16 + i] = count(i, i) * dot(blocks[NODE + i, 64:96], kernel)
        return 0

    lax.fori_loop(0, 8, own, 0)


def far_pair(scale, count, blocks, rows, fields, i, b):
    kernel = matern(scale, dot(rows[NODE + b], blocks[NODE + i]))
    fields[16 + i] += count(i, b) * dot(blocks[NODE + b, 64:96], kernel)
    fields[16 + b] += count(b, i) * dot_t(blocks[NODE + i, 64:96], kernel)


def near_leaf(scale, me, near, blocks, rows, fields, g):
    target = blocks[OWN + g]
    total = jnp.zeros((32, 256), f32)
    for k in range(16):
        leaf = near[g, k]
        offset = jnp.clip(leaf - (me - 1) * 16, 0, 47)
        place = jnp.where(leaf < 0, ZERO, jnp.where(offset >= 32, offset + 16, offset))
        kernel = matern(scale, dot(rows[place], target))
        total = total + dot(blocks[place, 64:96], kernel)
    fields[g] = total


def kernel(
    scale,
    devices,
    points,
    charges,
    order,
    near,
    far_list,
    local_skel,
    upper_skel,
    potentials,
    root,
    blocks,
    rows,
    kernels,
    source,
    fields,
    chain,
    chain_rows,
    chain_kernels,
    chain_fields,
    side_sent,
    side_got,
    up_sent,
    up_got,
):
    me = lax.axis_index("leaf")
    levels = devices.bit_length() - 1
    after, before = (me + 1) % devices, (me + devices - 1) % devices

    def bit_of(power):
        return (me // power) % 2

    def partner_of(power):
        return me + power * (1 - 2 * bit_of(power))

    barrier = pltpu.get_barrier_semaphore()
    others = [after, before] + [partner_of(2**r) for r in range(levels)]
    for other in others:
        pl.semaphore_signal(barrier, inc=1, device_id=(other,), device_id_type=MESH)
    blocks[ZERO] = jnp.zeros((128, 256), bf16)
    rows[ZERO] = jnp.zeros((256, 128), bf16)
    sort_in(points, charges, order, source, blocks, rows)
    pl.semaphore_wait(barrier, len(others))

    def side_copy(side, target, other):
        return pltpu.make_async_remote_copy(
            src_ref=blocks.at[pl.ds(OWN, 16)],
            dst_ref=blocks.at[pl.ds(target, 16)],
            send_sem=side_sent.at[side],
            recv_sem=side_got.at[side],
            device_id=(other,),
            device_id_type=MESH,
        )

    sides = [side_copy(0, LEFT, after), side_copy(1, RIGHT, before)]
    for side in sides:
        side.start()
    local_up(scale, local_skel, blocks, rows, kernels)

    def up_copy(r, power):
        own = bit_of(power)
        return pltpu.make_async_remote_copy(
            src_ref=chain.at[r, own],
            dst_ref=chain.at[r, own],
            send_sem=up_sent.at[r],
            recv_sem=up_got.at[r],
            device_id=(partner_of(power),),
            device_id_type=MESH,
        )

    def place(r, power, block, flat):
        chain[r, bit_of(power)] = block
        chain_rows[r, bit_of(power)] = flat

    def meet(r, power, last):
        own = bit_of(power)
        up_copy(r, power).wait()
        chain_rows[r, 1 - own] = rows_of(chain[r, 1 - own])
        kernel = matern(scale, dot(chain_rows[r, 1 - own], chain[r, own]))
        chain_fields[r] = dot(chain[r, 1 - own, 64:96], kernel)
        if not last:
            row = devices - devices // power + me // (2 * power)
            block, flat = lift(
                scale,
                chain[r, 0],
                chain[r, 1],
                chain_rows[r, 0],
                chain_rows[r, 1],
                upper_skel[pl.ds(row, 1), :],
                chain_kernels.at[r],
            )
            place(r + 1, 2 * power, block, flat)
            up_copy(r + 1, 2 * power).start()

    count = far_counts(far_list)

    def pairs(lo, hi, steps):
        def body(i, _):
            for step in steps:
                far_pair(scale, count, blocks, rows, fields, i, (i + step) % 8)
            return 0

        lax.fori_loop(lo, hi, body, 0)

    def leaves(lo, size):
        def body(g, _):
            near_leaf(scale, me, near, blocks, rows, fields, g)
            return 0

        lax.fori_loop(lo, lo + size, body, 0)

    place(0, 1, blocks[NODE + 14], rows[NODE + 14])
    up_copy(0, 1).start()
    for a in (8, 10, 12):
        couple_pair(scale, blocks, rows, fields, a, a + 1)
    meet(0, 1, False)
    far_own(scale, count, blocks, rows, fields)
    meet(1, 2, False)
    pairs(0, 8, (1, 2, 3))
    meet(2, 4, False)
    pairs(0, 4, (4,))
    for side in sides:
        side.wait()

    def side_rows(g, _):
        rows[LEFT + g] = rows_of(blocks[LEFT + g])
        rows[RIGHT + g] = rows_of(blocks[RIGHT + g])
        return 0

    lax.fori_loop(0, 16, side_rows, 0)

    def step(t, power):
        leaves(4 * t, 4)
        meet(t + 3, power, False)
        return 2 * power

    lax.fori_loop(0, 4, step, 8)
    meet(7, 128, True)
    for r in range(levels - 2, -1, -1):
        chain_fields[r] += pushed(chain_fields[r + 1], chain_kernels[r, bit_of(2**r)])
    root[0] = chain_fields[0]
    fields[30] = chain_fields[0]
    local_down(fields, kernels)
    sort_out(order, fields, potentials)


def solution(mesh):
    devices = mesh.shape["leaf"]

    def local(points, charges, order, near, far_list, local_skel, upper_skel):
        vmem = pl.BlockSpec(memory_space=pltpu.VMEM)
        smem = pl.BlockSpec(memory_space=pltpu.SMEM)
        return pl.pallas_call(
            functools.partial(kernel, 2.0 * math.sqrt(3.0 / 64), devices),
            out_shape=(
                jax.ShapeDtypeStruct((32, 4096), f32),
                jax.ShapeDtypeStruct((1, 32, 256), f32),
            ),
            in_specs=[vmem, vmem, vmem, smem, smem, vmem, vmem],
            out_specs=(vmem, vmem),
            scratch_shapes=[
                pltpu.VMEM((64, 128, 256), bf16),
                pltpu.VMEM((64, 256, 128), bf16),
                pltpu.VMEM((15, 2, 256, 256), bf16),
                pltpu.VMEM((16, 96, 256), bf16),
                pltpu.VMEM((31, 32, 256), f32),
                pltpu.VMEM((8, 2, 128, 256), bf16),
                pltpu.VMEM((8, 2, 256, 128), bf16),
                pltpu.VMEM((7, 2, 256, 256), bf16),
                pltpu.VMEM((8, 32, 256), f32),
                pltpu.SemaphoreType.DMA((2,)),
                pltpu.SemaphoreType.DMA((2,)),
                pltpu.SemaphoreType.DMA((8,)),
                pltpu.SemaphoreType.DMA((8,)),
            ],
            compiler_params=pltpu.CompilerParams(
                collective_id=0, has_side_effects=True, vmem_limit_bytes=60 << 20
            ),
            name="tree",
        )(points, charges, order, near, far_list, local_skel, upper_skel)

    placed = (
        P(None, "leaf"),
        P(None, "leaf"),
        P("leaf", None),
        P("leaf", None),
        P("leaf", None),
        P("leaf", None),
        P(),
    )
    return jax.shard_map(
        local,
        mesh=mesh,
        in_specs=placed,
        out_specs=(P(None, "leaf"), P("leaf", None, None)),
        check_vma=False,
    )
```

```python
import functools
import math

import jax
import jax.numpy as jnp
from jax import lax
from jax.experimental import pallas as pl
from jax.experimental.pallas import tpu as pltpu
from jax.sharding import PartitionSpec as P

f32 = jnp.float32
bf16 = jnp.bfloat16
MESH = pl.DeviceIdType.MESH
gain = math.sqrt(2.0)

LEFT, OWN, NODE, ZERO, RIGHT = 0, 16, 32, 47, 48


def dot(a, b):
    return jnp.dot(a, b, preferred_element_type=f32)


def dot_t(a, b):
    return lax.dot_general(a, b, (((1,), (1,)), ((), ())), preferred_element_type=f32)


def matern(scale, dist):
    positive = jnp.maximum(dist, 1e-30)
    radius = positive * lax.rsqrt(positive)
    return ((1.0 + radius * scale) * jnp.exp2(radius * (-scale * math.log2(math.e)))).astype(bf16)


def rows_of(block):
    columns = jnp.concatenate(
        [block[0:64] * -0.5, jnp.zeros((32, block.shape[1]), bf16), block[112:128], block[96:112]], axis=0
    )
    return columns.T


def block_of(stacked):
    coords = stacked[0:64]
    square = jnp.sum(coords * coords, axis=0, keepdims=True)
    high = square.astype(bf16).astype(f32)
    rest = square - high
    middle = rest.astype(bf16).astype(f32)
    low = rest - middle
    place = lax.broadcasted_iota(jnp.int32, (16, stacked.shape[1]), 0)
    ones = jnp.where(place < 3, 1.0, 0.0)
    terms = jnp.where(place == 0, high, jnp.where(place == 1, middle, jnp.where(place == 2, low, 0.0)))
    return jnp.concatenate([coords * -2.0, stacked[64:96], ones, terms], axis=0).astype(bf16)


def one_hot(chosen, first, height=256):
    place = lax.broadcasted_iota(jnp.int32, (height, chosen.shape[1]), 0)
    return jnp.where(place == chosen - first, 1.0, 0.0).astype(bf16)


def stream(scale, stage, jobs):
    for k in range(len(jobs) + 1):
        if k < len(jobs):
            source, target = jobs[k][0](), jobs[k][1]()
            for c in (0, 128):
                stage[k % 2, c : c + 128] = matern(scale, dot(source[c : c + 128], target))
        if k > 0:
            jobs[k - 1][2](stage.at[(k - 1) % 2])


def lift_many(scale, nodes):
    targets = []
    for left, right, _, _, chosen, _, out, out_rows in nodes:
        picked = dot(left[...], one_hot(chosen, 0)) + dot(right[...], one_hot(chosen, 256))
        target = picked.astype(bf16)
        targets.append(target)
        out[...] = target
        out_rows[...] = rows_of(target)
    halves = [(i, h) for i in range(len(nodes)) for h in range(2)]
    sums = [None] * len(nodes)

    def use(i, h):
        part = dot(nodes[i][h][64:112], nodes[i][5][h])
        sums[i] = part if h == 0 else sums[i] + part
        if h == 1:
            nodes[i][6][64:96] = (gain * (sums[i][0:32] / sums[i][32:33])).astype(bf16)

    for k, (i, h) in enumerate(halves):
        source = nodes[i][2 + h]
        for c in (0, 128):
            nodes[i][5][h, c : c + 128] = matern(scale, dot(source[c : c + 128], targets[i]))
        if k > 0:
            use(*halves[k - 1])
    use(*halves[-1])


def pushed(field, kernel):
    high = jnp.concatenate([field.astype(bf16), jnp.ones((16, field.shape[1]), bf16)], axis=0)
    sums = dot_t(high, kernel)
    return sums[0:32] / sums[32:33]


def sort_in(points, charges, order, source, blocks, rows):
    def fill(b, _):
        lanes = pl.ds(pl.multiple_of(b * 256, 256), 256)
        source[b, 0:64] = points[:, lanes]
        source[b, 64:96] = charges[:, lanes]
        return 0

    lax.fori_loop(0, 16, fill, 0)

    def leaf(g):
        ids = order[:, pl.ds(pl.multiple_of(g * 256, 256), 256)]
        picks = one_hot(ids & 255, 0)
        high = ids >> 8
        stacked = None
        for part in range(SPLIT_IN):
            size = 16 // SPLIT_IN
            found = dot(source[part * size : part * size + size].reshape(size * 96, 256), picks)
            for b in range(size):
                piece = found[b * 96 : b * 96 + 96]
                stacked = piece if stacked is None else jnp.where(high == part * size + b, piece, stacked)
        block = block_of(stacked)
        blocks[OWN + g] = block
        rows[OWN + g] = rows_of(block)

    def some(p, _):
        for q in range(UNROLL_IN):
            leaf(UNROLL_IN * p + q)
        return 0

    lax.fori_loop(0, 16 // UNROLL_IN, some, 0)


SPLIT_IN = 4
UNROLL_IN = 4
UNROLL_OUT = 4
PARTS_OUT = 4
UP_BATCHES = ((0, 1, 2, 3), (4, 5, 6, 7), (8, 9, 10, 11), (12, 13), (14,))


def sort_out(order, fields, output):
    output[...] = jnp.zeros_like(output)

    def some(p, _):
        highs, picks, terms = [], [], []
        for q in range(UNROLL_OUT):
            g = UNROLL_OUT * p + q
            ids = order[:, pl.ds(pl.multiple_of(g * 256, 256), 256)]
            hot = one_hot(ids & 255, 0)
            value = fields[g]
            first = value.astype(bf16)
            second = (value - first.astype(f32)).astype(bf16)
            highs += [ids >> 8]
            picks += [hot, hot]
            terms += [[first, second]]
        picks = jnp.concatenate(picks, axis=1)
        size = 16 // PARTS_OUT
        for part in range(PARTS_OUT):
            masked = []
            for b in range(part * size, part * size + size):
                row = []
                for q in range(UNROLL_OUT):
                    mask = jnp.where(highs[q] == b, 1.0, 0.0).astype(bf16)
                    row += [terms[q][0] * mask, terms[q][1] * mask]
                masked.append(jnp.concatenate(row, axis=1))
            found = dot_t(jnp.concatenate(masked, axis=0), picks)
            for b in range(size):
                lanes = slice((part * size + b) * 256, (part * size + b + 1) * 256)
                output[:, lanes] += found[b * 32 : b * 32 + 32]
        return 0

    lax.fori_loop(0, 16 // UNROLL_OUT, some, 0)


def local_up(scale, skel, blocks, rows, kernels):
    for batch in UP_BATCHES:
        lift_many(
            scale,
            [
                (
                    blocks.at[OWN + 2 * n],
                    blocks.at[OWN + 1 + 2 * n],
                    rows.at[OWN + 2 * n],
                    rows.at[OWN + 1 + 2 * n],
                    skel[n : n + 1, :],
                    kernels.at[n],
                    blocks.at[NODE + n],
                    rows.at[NODE + n],
                )
                for n in batch
            ],
        )


def local_down(fields, kernels):
    def one(n):
        field = fields[16 + n]
        fields[2 * n] += pushed(field, kernels[n, 0])
        fields[2 * n + 1] += pushed(field, kernels[n, 1])

    one(14)

    def two(p, _):
        one(13 - 2 * p)
        one(12 - 2 * p)
        return 0

    lax.fori_loop(0, 7, two, 0)


def far(scale, far_list, blocks, rows, fields, stage, pairs):
    def count(i, b):
        total = 1.0 if b == i ^ 1 else 0.0
        for e in range(8):
            total = total + jnp.where(far_list[i, e] == b, 1.0, 0.0)
        return total

    def use(i, b, kernel):
        fields[16 + i] += count(i, b) * dot(blocks[NODE + b, 64:96], kernel[...])
        if i != b:
            fields[16 + b] += count(b, i) * dot_t(blocks[NODE + i, 64:96], kernel[...])

    jobs = [
        (
            functools.partial(lambda b: rows[NODE + b], b),
            functools.partial(lambda i: blocks[NODE + i], i),
            functools.partial(use, i, b),
        )
        for i, b in pairs
    ]
    stream(scale, stage, jobs)


def couple(scale, blocks, rows, fields, stage, pairs):
    def use(a, b, kernel):
        fields[16 + b] = dot(blocks[NODE + a, 64:96], kernel[...])
        fields[16 + a] = dot_t(blocks[NODE + b, 64:96], kernel[...])

    jobs = [
        (
            functools.partial(lambda a: rows[NODE + a], a),
            functools.partial(lambda b: blocks[NODE + b], b),
            functools.partial(use, a, b),
        )
        for a, b in pairs
    ]
    stream(scale, stage, jobs)


FAR_PAIRS = [(i, i) for i in range(8)] + [(i, i ^ d) for d in range(1, 8) for i in range(8) if i < i ^ d]


def near_steps(scale, me, near, blocks, rows, fields, stage, g):
    target = blocks[OWN + g]
    total = [jnp.zeros((32, 256), f32)]

    def place(k):
        leaf = near[g, k]
        offset = jnp.clip(leaf - (me - 1) * 16, 0, 47)
        return jnp.where(leaf < 0, ZERO, jnp.where(offset >= 32, offset + 16, offset))

    places = [place(k) for k in range(16)]

    def one(k):
        if k < 16:
            for c in (0, 128):
                stage[k % 2, c : c + 128] = matern(scale, dot(rows[places[k], c : c + 128], target))
        if k > 0:
            total[0] = total[0] + dot(blocks[places[k - 1], 64:96], stage[(k - 1) % 2])
        if k == 16:
            fields[g] = total[0]

    return [functools.partial(one, k) for k in range(17)]


def run(steps, others=(), every=2):
    others = list(others)
    for k, step in enumerate(steps):
        step()
        if others and k % every == 0:
            others.pop(0)()
    for other in others:
        other()


def kernel(
    scale,
    devices,
    points,
    charges,
    order,
    near,
    far_list,
    local_skel,
    upper_skel,
    potentials,
    root,
    blocks,
    rows,
    kernels,
    source,
    fields,
    chain,
    chain_rows,
    chain_kernels,
    chain_fields,
    stage,
    chain_stage,
    side_sent,
    side_got,
    up_sent,
    up_got,
):
    me = lax.axis_index("leaf")
    levels = devices.bit_length() - 1
    after, before = (me + 1) % devices, (me + devices - 1) % devices

    def bit_of(power):
        return (me // power) % 2

    def partner_of(power):
        return me + power * (1 - 2 * bit_of(power))

    barrier = pltpu.get_barrier_semaphore()
    others = [after, before] + [partner_of(2**r) for r in range(levels)]
    for other in others:
        pl.semaphore_signal(barrier, inc=1, device_id=(other,), device_id_type=MESH)
    blocks[ZERO] = jnp.zeros((128, 256), bf16)
    rows[ZERO] = jnp.zeros((256, 128), bf16)
    sort_in(points, charges, order, source, blocks, rows)
    pl.semaphore_wait(barrier, len(others))

    def side_copy(side, target, other):
        return pltpu.make_async_remote_copy(
            src_ref=blocks.at[pl.ds(OWN, 16)],
            dst_ref=blocks.at[pl.ds(target, 16)],
            send_sem=side_sent.at[side],
            recv_sem=side_got.at[side],
            device_id=(other,),
            device_id_type=MESH,
        )

    sides = [side_copy(0, LEFT, after), side_copy(1, RIGHT, before)]
    for side in sides:
        side.start()
    local_up(scale, local_skel, blocks, rows, kernels)

    def up_copy(r, power):
        own = bit_of(power)
        return pltpu.make_async_remote_copy(
            src_ref=chain.at[r, own],
            dst_ref=chain.at[r, own],
            send_sem=up_sent.at[r],
            recv_sem=up_got.at[r],
            device_id=(partner_of(power),),
            device_id_type=MESH,
        )

    def place(r, power, block, flat):
        chain[r, bit_of(power)] = block
        chain_rows[r, bit_of(power)] = flat

    def meet_steps(r, power, last):
        own = bit_of(power)
        kept = {}

        def sibling():
            chain_rows[r, 1 - own] = rows_of(chain[r, 1 - own])

        def pick():
            row = devices - devices // power + me // (2 * power)
            chosen = upper_skel[pl.ds(row, 1), :]
            picked = dot(chain[r, 0], one_hot(chosen, 0)) + dot(chain[r, 1], one_hot(chosen, 256))
            kept["target"] = picked.astype(bf16)

        def flat():
            chain_rows[r + 1, bit_of(2 * power)] = rows_of(kept["target"])

        def half(h):
            for c in (0, 128):
                piece = matern(scale, dot(chain_rows[r, h, c : c + 128], kept["target"]))
                chain_kernels[r, h, c : c + 128] = piece

        def weigh():
            sums = dot(chain[r, 0, 64:112], chain_kernels[r, 0])
            sums = sums + dot(chain[r, 1, 64:112], chain_kernels[r, 1])
            weights = (gain * (sums[0:32] / sums[32:33])).astype(bf16)
            target = kept["target"]
            chain[r + 1, bit_of(2 * power)] = jnp.concatenate(
                [target[0:64], weights, target[96:128]], axis=0
            )

        def couple_kernel():
            for c in (0, 128):
                chain_stage[c : c + 128] = matern(
                    scale, dot(chain_rows[r, 1 - own, c : c + 128], chain[r, own])
                )

        def couple_use():
            chain_fields[r] = dot(chain[r, 1 - own, 64:96], chain_stage[...])

        if last:
            return [sibling, couple_kernel, couple_use]
        return [
            sibling,
            pick,
            functools.partial(half, 0),
            functools.partial(half, 1),
            weigh,
            flat,
            couple_kernel,
            couple_use,
        ]

    def down(r):
        chain_fields[r] += pushed(chain_fields[r + 1], chain_kernels[r, bit_of(2**r)])

    def leaf(g):
        return near_steps(scale, me, near, blocks, rows, fields, stage, g)

    chain[0, bit_of(1)] = blocks[NODE + 14]
    chain_rows[0, bit_of(1)] = rows[NODE + 14]
    up_copy(0, 1).start()
    fields[16:24] = jnp.zeros((8, 32, 256), f32)
    couple(scale, blocks, rows, fields, stage, [(8, 9), (10, 11), (12, 13)])
    far(scale, far_list, blocks, rows, fields, stage, FAR_PAIRS)
    for side in sides:
        side.wait()

    def side_rows(g, _):
        rows[LEFT + g] = rows_of(blocks[LEFT + g])
        rows[RIGHT + g] = rows_of(blocks[RIGHT + g])
        return 0

    lax.fori_loop(0, 16, side_rows, 0)

    def step(r, power):
        run(leaf(2 * r))
        up_copy(r, power).wait()
        run(leaf(2 * r + 1), meet_steps(r, power, False))
        up_copy(r + 1, 2 * power).start()
        return 2 * power

    lax.fori_loop(0, levels - 1, step, 1)
    run(leaf(14))
    up_copy(levels - 1, devices // 2).wait()
    downs = [functools.partial(down, r) for r in range(levels - 2, -1, -1)]
    run(leaf(15), meet_steps(levels - 1, devices // 2, True) + downs, every=1)
    root[0] = chain_fields[0]
    fields[30] = chain_fields[0]
    local_down(fields, kernels)
    sort_out(order, fields, potentials)


def solution(mesh):
    devices = mesh.shape["leaf"]

    def local(points, charges, order, near, far_list, local_skel, upper_skel):
        vmem = pl.BlockSpec(memory_space=pltpu.VMEM)
        smem = pl.BlockSpec(memory_space=pltpu.SMEM)
        return pl.pallas_call(
            functools.partial(kernel, 2.0 * math.sqrt(3.0 / 64), devices),
            out_shape=(
                jax.ShapeDtypeStruct((32, 4096), f32),
                jax.ShapeDtypeStruct((1, 32, 256), f32),
            ),
            in_specs=[vmem, vmem, vmem, smem, smem, vmem, vmem],
            out_specs=(vmem, vmem),
            scratch_shapes=[
                pltpu.VMEM((64, 128, 256), bf16),
                pltpu.VMEM((64, 256, 128), bf16),
                pltpu.VMEM((15, 2, 256, 256), bf16),
                pltpu.VMEM((16, 96, 256), bf16),
                pltpu.VMEM((31, 32, 256), f32),
                pltpu.VMEM((8, 2, 128, 256), bf16),
                pltpu.VMEM((8, 2, 256, 128), bf16),
                pltpu.VMEM((7, 2, 256, 256), bf16),
                pltpu.VMEM((8, 32, 256), f32),
                pltpu.VMEM((2, 256, 256), bf16),
                pltpu.VMEM((256, 256), bf16),
                pltpu.SemaphoreType.DMA((2,)),
                pltpu.SemaphoreType.DMA((2,)),
                pltpu.SemaphoreType.DMA((8,)),
                pltpu.SemaphoreType.DMA((8,)),
            ],
            compiler_params=pltpu.CompilerParams(
                collective_id=0, has_side_effects=True, vmem_limit_bytes=60 << 20
            ),
            name="tree",
        )(points, charges, order, near, far_list, local_skel, upper_skel)

    placed = (
        P(None, "leaf"),
        P(None, "leaf"),
        P("leaf", None),
        P("leaf", None),
        P("leaf", None),
        P("leaf", None),
        P(),
    )
    return jax.shard_map(
        local,
        mesh=mesh,
        in_specs=placed,
        out_specs=(P(None, "leaf"), P("leaf", None, None)),
        check_vma=False,
    )
```

```python
import functools
import math

import jax
import jax.numpy as jnp
from jax import lax
from jax.experimental import pallas as pl
from jax.experimental.pallas import tpu as pltpu
from jax.sharding import PartitionSpec as P

f32 = jnp.float32
bf16 = jnp.bfloat16
MESH = pl.DeviceIdType.MESH
gain = math.sqrt(2.0)

LEFT, OWN, NODE, ZERO, RIGHT = 0, 16, 32, 47, 48


def dot(a, b):
    return jnp.dot(a, b, preferred_element_type=f32)


def dot_t(a, b):
    return lax.dot_general(a, b, (((1,), (1,)), ((), ())), preferred_element_type=f32)


def matern(scale, dist):
    positive = jnp.maximum(dist, 1e-30)
    radius = positive * lax.rsqrt(positive)
    return ((1.0 + radius * scale) * jnp.exp2(radius * (-scale * math.log2(math.e)))).astype(bf16)


def rows_of(block):
    columns = jnp.concatenate(
        [block[0:64] * -0.5, jnp.zeros((32, block.shape[1]), bf16), block[112:128], block[96:112]], axis=0
    )
    return columns.T


def tail_of(coords):
    square = jnp.sum(coords * coords, axis=0, keepdims=True)
    high = square.astype(bf16).astype(f32)
    rest = square - high
    middle = rest.astype(bf16).astype(f32)
    low = rest - middle
    place = lax.broadcasted_iota(jnp.int32, (16, coords.shape[1]), 0)
    ones = jnp.where(place < 3, 1.0, 0.0)
    terms = jnp.where(place == 0, high, jnp.where(place == 1, middle, jnp.where(place == 2, low, 0.0)))
    return jnp.concatenate([ones, terms], axis=0).astype(bf16)


def block_of(stacked):
    coords = stacked[0:64]
    whole = jnp.concatenate([coords * -2.0, stacked[64:96]], axis=0).astype(bf16)
    return jnp.concatenate([whole, tail_of(coords)], axis=0)


def complete(block, rows):
    block[96:128] = tail_of(block[0:64].astype(f32) * -0.5)
    rows[...] = rows_of(block[...])


def one_hot(chosen, first, height=256):
    place = lax.broadcasted_iota(jnp.int32, (height, chosen.shape[1]), 0)
    return jnp.where(place == chosen - first, 1.0, 0.0).astype(bf16)


def stream(scale, stage, jobs):
    for k in range(len(jobs) + 1):
        if k < len(jobs):
            source, target = jobs[k][0](), jobs[k][1]()
            for c in (0, 128):
                stage[k % 2, c : c + 128] = matern(scale, dot(source[c : c + 128], target))
        if k > 0:
            jobs[k - 1][2](stage.at[(k - 1) % 2])


def lift_many(scale, nodes):
    targets = []
    for left, right, _, _, chosen, _, out, out_rows in nodes:
        picked = dot(left[...], one_hot(chosen, 0)) + dot(right[...], one_hot(chosen, 256))
        target = picked.astype(bf16)
        targets.append(target)
        out[...] = target
        out_rows[...] = rows_of(target)
    halves = [(i, h) for i in range(len(nodes)) for h in range(2)]
    sums = [None] * len(nodes)

    def use(i, h):
        part = dot(nodes[i][h][64:112], nodes[i][5][h])
        sums[i] = part if h == 0 else sums[i] + part
        if h == 1:
            nodes[i][6][64:96] = (gain * (sums[i][0:32] / sums[i][32:33])).astype(bf16)

    for k, (i, h) in enumerate(halves):
        source = nodes[i][2 + h]
        for c in (0, 128):
            nodes[i][5][h, c : c + 128] = matern(scale, dot(source[c : c + 128], targets[i]))
        if k > 0:
            use(*halves[k - 1])
    use(*halves[-1])


def pushed(field, kernel):
    high = jnp.concatenate([field.astype(bf16), jnp.ones((16, field.shape[1]), bf16)], axis=0)
    sums = dot_t(high, kernel)
    return sums[0:32] / sums[32:33]


def sort_in(points, charges, order, source, blocks, rows):
    def fill(b, _):
        lanes = pl.ds(pl.multiple_of(b * 256, 256), 256)
        source[b, 0:64] = points[:, lanes]
        source[b, 64:96] = charges[:, lanes]
        return 0

    lax.fori_loop(0, 16, fill, 0)

    def leaf(g):
        ids = order[:, pl.ds(pl.multiple_of(g * 256, 256), 256)]
        picks = one_hot(ids & 255, 0)
        high = ids >> 8
        stacked = None
        for part in range(SPLIT_IN):
            size = 16 // SPLIT_IN
            found = dot(source[part * size : part * size + size].reshape(size * 96, 256), picks)
            for b in range(size):
                piece = found[b * 96 : b * 96 + 96]
                stacked = piece if stacked is None else jnp.where(high == part * size + b, piece, stacked)
        block = block_of(stacked)
        blocks[OWN + g] = block
        rows[OWN + g] = rows_of(block)

    def some(p, _):
        for q in range(UNROLL_IN):
            leaf(UNROLL_IN * p + q)
        return 0

    lax.fori_loop(0, 16 // UNROLL_IN, some, 0)


SPLIT_IN = 4
UNROLL_IN = 4
UNROLL_OUT = 4
PARTS_OUT = 4
UP_BATCHES = ((0, 1, 2, 3), (4, 5, 6, 7), (8, 9, 10, 11), (12, 13), (14,))


def sort_out(order, fields, output):
    output[...] = jnp.zeros_like(output)

    def some(p, _):
        highs, picks, terms = [], [], []
        for q in range(UNROLL_OUT):
            g = UNROLL_OUT * p + q
            ids = order[:, pl.ds(pl.multiple_of(g * 256, 256), 256)]
            hot = one_hot(ids & 255, 0)
            value = fields[g]
            first = value.astype(bf16)
            second = (value - first.astype(f32)).astype(bf16)
            highs += [ids >> 8]
            picks += [hot, hot]
            terms += [[first, second]]
        picks = jnp.concatenate(picks, axis=1)
        size = 16 // PARTS_OUT
        for part in range(PARTS_OUT):
            masked = []
            for b in range(part * size, part * size + size):
                row = []
                for q in range(UNROLL_OUT):
                    mask = jnp.where(highs[q] == b, 1.0, 0.0).astype(bf16)
                    row += [terms[q][0] * mask, terms[q][1] * mask]
                masked.append(jnp.concatenate(row, axis=1))
            found = dot_t(jnp.concatenate(masked, axis=0), picks)
            for b in range(size):
                lanes = slice((part * size + b) * 256, (part * size + b + 1) * 256)
                output[:, lanes] += found[b * 32 : b * 32 + 32]
        return 0

    lax.fori_loop(0, 16 // UNROLL_OUT, some, 0)


def local_up(scale, skel, blocks, rows, kernels):
    for batch in UP_BATCHES:
        lift_many(
            scale,
            [
                (
                    blocks.at[OWN + 2 * n],
                    blocks.at[OWN + 1 + 2 * n],
                    rows.at[OWN + 2 * n],
                    rows.at[OWN + 1 + 2 * n],
                    skel[n : n + 1, :],
                    kernels.at[n],
                    blocks.at[NODE + n],
                    rows.at[NODE + n],
                )
                for n in batch
            ],
        )


def local_down(fields, kernels):
    def one(n):
        field = fields[16 + n]
        fields[2 * n] += pushed(field, kernels[n, 0])
        fields[2 * n + 1] += pushed(field, kernels[n, 1])

    one(14)

    def two(p, _):
        one(13 - 2 * p)
        one(12 - 2 * p)
        return 0

    lax.fori_loop(0, 7, two, 0)


def far(scale, far_list, blocks, rows, fields, stage, pairs):
    def count(i, b):
        total = 1.0 if b == i ^ 1 else 0.0
        for e in range(8):
            total = total + jnp.where(far_list[i, e] == b, 1.0, 0.0)
        return total

    def use(i, b, kernel):
        fields[16 + i] += count(i, b) * dot(blocks[NODE + b, 64:96], kernel[...])
        if i != b:
            fields[16 + b] += count(b, i) * dot_t(blocks[NODE + i, 64:96], kernel[...])

    jobs = [
        (
            functools.partial(lambda b: rows[NODE + b], b),
            functools.partial(lambda i: blocks[NODE + i], i),
            functools.partial(use, i, b),
        )
        for i, b in pairs
    ]
    stream(scale, stage, jobs)


def couple(scale, blocks, rows, fields, stage, pairs):
    def use(a, b, kernel):
        fields[16 + b] = dot(blocks[NODE + a, 64:96], kernel[...])
        fields[16 + a] = dot_t(blocks[NODE + b, 64:96], kernel[...])

    jobs = [
        (
            functools.partial(lambda a: rows[NODE + a], a),
            functools.partial(lambda b: blocks[NODE + b], b),
            functools.partial(use, a, b),
        )
        for a, b in pairs
    ]
    stream(scale, stage, jobs)


FAR_PAIRS = [(i, i) for i in range(8)] + [(i, i ^ d) for d in range(1, 8) for i in range(8) if i < i ^ d]


def near_steps(scale, me, near, blocks, rows, fields, stage, g):
    target = blocks[OWN + g]
    total = [jnp.zeros((32, 256), f32)]

    def place(k):
        leaf = near[g, k]
        offset = jnp.clip(leaf - (me - 1) * 16, 0, 47)
        return jnp.where(leaf < 0, ZERO, jnp.where(offset >= 32, offset + 16, offset))

    places = [place(k) for k in range(16)]

    def one(k):
        if k < 16:
            for c in (0, 128):
                stage[k % 2, c : c + 128] = matern(scale, dot(rows[places[k], c : c + 128], target))
        if k > 0:
            total[0] = total[0] + dot(blocks[places[k - 1], 64:96], stage[(k - 1) % 2])
        if k == 16:
            fields[g] = total[0]

    return [functools.partial(one, k) for k in range(17)]


def run(steps, others=(), every=2):
    others = list(others)
    for k, step in enumerate(steps):
        step()
        if others and k % every == 0:
            others.pop(0)()
    for other in others:
        other()


def kernel(
    scale,
    devices,
    points,
    charges,
    order,
    near,
    far_list,
    local_skel,
    upper_skel,
    potentials,
    root,
    blocks,
    rows,
    kernels,
    source,
    fields,
    chain,
    chain_rows,
    chain_kernels,
    chain_fields,
    stage,
    chain_stage,
    side_sent,
    side_got,
    up_sent,
    up_got,
):
    me = lax.axis_index("leaf")
    levels = devices.bit_length() - 1
    after, before = (me + 1) % devices, (me + devices - 1) % devices

    def bit_of(power):
        return (me // power) % 2

    def partner_of(power):
        return me + power * (1 - 2 * bit_of(power))

    barrier = pltpu.get_barrier_semaphore()
    others = [after, before] + [partner_of(2**r) for r in range(levels)]
    for other in others:
        pl.semaphore_signal(barrier, inc=1, device_id=(other,), device_id_type=MESH)
    blocks[ZERO] = jnp.zeros((128, 256), bf16)
    rows[ZERO] = jnp.zeros((256, 128), bf16)
    sort_in(points, charges, order, source, blocks, rows)
    pl.semaphore_wait(barrier, len(others))

    def side_copy(side, target, other):
        return pltpu.make_async_remote_copy(
            src_ref=blocks.at[pl.ds(OWN, 16), 0:96],
            dst_ref=blocks.at[pl.ds(target, 16), 0:96],
            send_sem=side_sent.at[side],
            recv_sem=side_got.at[side],
            device_id=(other,),
            device_id_type=MESH,
        )

    sides = [side_copy(0, LEFT, after), side_copy(1, RIGHT, before)]
    for side in sides:
        side.start()
    local_up(scale, local_skel, blocks, rows, kernels)

    def up_copy(r, power):
        own = bit_of(power)
        return pltpu.make_async_remote_copy(
            src_ref=chain.at[r, own, 0:96],
            dst_ref=chain.at[r, own, 0:96],
            send_sem=up_sent.at[r],
            recv_sem=up_got.at[r],
            device_id=(partner_of(power),),
            device_id_type=MESH,
        )

    def place(r, power, block, flat):
        chain[r, bit_of(power)] = block
        chain_rows[r, bit_of(power)] = flat

    def meet_steps(r, power, last):
        own = bit_of(power)
        kept = {}

        def sibling():
            complete(chain.at[r, 1 - own], chain_rows.at[r, 1 - own])

        def pick():
            row = devices - devices // power + me // (2 * power)
            chosen = upper_skel[pl.ds(row, 1), :]
            picked = dot(chain[r, 0], one_hot(chosen, 0)) + dot(chain[r, 1], one_hot(chosen, 256))
            kept["target"] = picked.astype(bf16)

        def flat():
            chain_rows[r + 1, bit_of(2 * power)] = rows_of(kept["target"])

        def half(h):
            for c in (0, 128):
                piece = matern(scale, dot(chain_rows[r, h, c : c + 128], kept["target"]))
                chain_kernels[r, h, c : c + 128] = piece

        def weigh():
            sums = dot(chain[r, 0, 64:112], chain_kernels[r, 0])
            sums = sums + dot(chain[r, 1, 64:112], chain_kernels[r, 1])
            weights = (gain * (sums[0:32] / sums[32:33])).astype(bf16)
            target = kept["target"]
            chain[r + 1, bit_of(2 * power)] = jnp.concatenate(
                [target[0:64], weights, target[96:128]], axis=0
            )

        def couple_kernel():
            for c in (0, 128):
                chain_stage[c : c + 128] = matern(
                    scale, dot(chain_rows[r, 1 - own, c : c + 128], chain[r, own])
                )

        def couple_use():
            chain_fields[r] = dot(chain[r, 1 - own, 64:96], chain_stage[...])

        if last:
            return [sibling, couple_kernel, couple_use]
        return [
            sibling,
            pick,
            functools.partial(half, 0),
            functools.partial(half, 1),
            couple_kernel,
            weigh,
            flat,
            couple_use,
        ]

    def down(r):
        chain_fields[r] += pushed(chain_fields[r + 1], chain_kernels[r, bit_of(2**r)])

    def leaf(g):
        return near_steps(scale, me, near, blocks, rows, fields, stage, g)

    chain[0, bit_of(1)] = blocks[NODE + 14]
    chain_rows[0, bit_of(1)] = rows[NODE + 14]
    up_copy(0, 1).start()
    def meet(r, power):
        up_copy(r, power).wait()
        run(meet_steps(r, power, False))
        up_copy(r + 1, 2 * power).start()

    fields[16:24] = jnp.zeros((8, 32, 256), f32)
    couple(scale, blocks, rows, fields, stage, [(8, 9), (10, 11), (12, 13)])
    meet(0, 1)
    far(scale, far_list, blocks, rows, fields, stage, FAR_PAIRS)
    meet(1, 2)
    for side in sides:
        side.wait()

    def side_rows(g, _):
        complete(blocks.at[LEFT + g], rows.at[LEFT + g])
        complete(blocks.at[RIGHT + g], rows.at[RIGHT + g])
        return 0

    lax.fori_loop(0, 16, side_rows, 0)

    def some(g, _):
        run(leaf(g))
        return 0

    def step(r, power):
        lo = jnp.where(r < 3, 0, jnp.where(r < 4, 1, jnp.where(r < 5, 3, jnp.where(r < 6, 6, 11))))
        hi = jnp.where(r < 3, 1, jnp.where(r < 4, 3, jnp.where(r < 5, 6, jnp.where(r < 6, 11, 13))))
        lax.fori_loop(lo, hi, some, 0)
        meet(r, power)
        return 2 * power

    lax.fori_loop(2, levels - 1, step, 4)
    lax.fori_loop(13, 15, some, 0)
    up_copy(levels - 1, devices // 2).wait()
    downs = [functools.partial(down, r) for r in range(levels - 2, -1, -1)]
    run(leaf(15), meet_steps(levels - 1, devices // 2, True) + downs, every=1)
    root[0] = chain_fields[0]
    fields[30] = chain_fields[0]
    local_down(fields, kernels)
    sort_out(order, fields, potentials)


def solution(mesh):
    devices = mesh.shape["leaf"]

    def local(points, charges, order, near, far_list, local_skel, upper_skel):
        vmem = pl.BlockSpec(memory_space=pltpu.VMEM)
        smem = pl.BlockSpec(memory_space=pltpu.SMEM)
        return pl.pallas_call(
            functools.partial(kernel, 2.0 * math.sqrt(3.0 / 64), devices),
            out_shape=(
                jax.ShapeDtypeStruct((32, 4096), f32),
                jax.ShapeDtypeStruct((1, 32, 256), f32),
            ),
            in_specs=[vmem, vmem, vmem, smem, smem, vmem, vmem],
            out_specs=(vmem, vmem),
            scratch_shapes=[
                pltpu.VMEM((64, 128, 256), bf16),
                pltpu.VMEM((64, 256, 128), bf16),
                pltpu.VMEM((15, 2, 256, 256), bf16),
                pltpu.VMEM((16, 96, 256), bf16),
                pltpu.VMEM((31, 32, 256), f32),
                pltpu.VMEM((8, 2, 128, 256), bf16),
                pltpu.VMEM((8, 2, 256, 128), bf16),
                pltpu.VMEM((7, 2, 256, 256), bf16),
                pltpu.VMEM((8, 32, 256), f32),
                pltpu.VMEM((2, 256, 256), bf16),
                pltpu.VMEM((256, 256), bf16),
                pltpu.SemaphoreType.DMA((2,)),
                pltpu.SemaphoreType.DMA((2,)),
                pltpu.SemaphoreType.DMA((8,)),
                pltpu.SemaphoreType.DMA((8,)),
            ],
            compiler_params=pltpu.CompilerParams(
                collective_id=0, has_side_effects=True, vmem_limit_bytes=60 << 20
            ),
            name="tree",
        )(points, charges, order, near, far_list, local_skel, upper_skel)

    placed = (
        P(None, "leaf"),
        P(None, "leaf"),
        P("leaf", None),
        P("leaf", None),
        P("leaf", None),
        P("leaf", None),
        P(),
    )
    return jax.shard_map(
        local,
        mesh=mesh,
        in_specs=placed,
        out_specs=(P(None, "leaf"), P("leaf", None, None)),
        check_vma=False,
    )
```

```python
import functools
import math

import jax
import jax.numpy as jnp
from jax import lax
from jax.experimental import pallas as pl
from jax.experimental.pallas import tpu as pltpu
from jax.sharding import PartitionSpec as P

f32 = jnp.float32
bf16 = jnp.bfloat16
MESH = pl.DeviceIdType.MESH
gain = math.sqrt(2.0)

LEFT, OWN, NODE, ZERO, RIGHT = 0, 16, 32, 47, 48


def dot(a, b):
    return jnp.dot(a, b, preferred_element_type=f32)


def dot_t(a, b):
    return lax.dot_general(a, b, (((1,), (1,)), ((), ())), preferred_element_type=f32)


def matern(scale, dist):
    positive = jnp.maximum(dist, 1e-30)
    radius = positive * lax.rsqrt(positive)
    return ((1.0 + radius * scale) * jnp.exp2(radius * (-scale * math.log2(math.e)))).astype(bf16)


def rows_of(block):
    columns = jnp.concatenate(
        [block[0:64] * -0.5, jnp.zeros((32, block.shape[1]), bf16), block[112:128], block[96:112]], axis=0
    )
    return columns.T


def tail_of(coords):
    square = jnp.sum(coords * coords, axis=0, keepdims=True)
    high = square.astype(bf16).astype(f32)
    rest = square - high
    middle = rest.astype(bf16).astype(f32)
    low = rest - middle
    place = lax.broadcasted_iota(jnp.int32, (16, coords.shape[1]), 0)
    ones = jnp.where(place < 3, 1.0, 0.0)
    terms = jnp.where(place == 0, high, jnp.where(place == 1, middle, jnp.where(place == 2, low, 0.0)))
    return jnp.concatenate([ones, terms], axis=0).astype(bf16)


def block_of(stacked):
    coords = stacked[0:64]
    whole = jnp.concatenate([coords * -2.0, stacked[64:96]], axis=0).astype(bf16)
    return jnp.concatenate([whole, tail_of(coords)], axis=0)


def complete(block, rows):
    block[96:128] = tail_of(block[0:64].astype(f32) * -0.5)
    rows[...] = rows_of(block[...])


def one_hot(chosen, first, height=256):
    place = lax.broadcasted_iota(jnp.int32, (height, chosen.shape[1]), 0)
    return jnp.where(place == chosen - first, 1.0, 0.0).astype(bf16)


def stream(scale, stage, jobs):
    for k in range(len(jobs) + 1):
        if k < len(jobs):
            source, target = jobs[k][0](), jobs[k][1]()
            for c in (0, 128):
                stage[k % 2, c : c + 128] = matern(scale, dot(source[c : c + 128], target))
        if k > 0:
            jobs[k - 1][2](stage.at[(k - 1) % 2])


def lift_many(scale, nodes):
    targets = []
    for left, right, _, _, chosen, _, out, out_rows in nodes:
        picked = dot(left[...], one_hot(chosen, 0)) + dot(right[...], one_hot(chosen, 256))
        target = picked.astype(bf16)
        targets.append(target)
        out[...] = target
        out_rows[...] = rows_of(target)
    halves = [(i, h) for i in range(len(nodes)) for h in range(2)]
    sums = [None] * len(nodes)

    def use(i, h):
        part = dot(nodes[i][h][64:112], nodes[i][5][h])
        sums[i] = part if h == 0 else sums[i] + part
        if h == 1:
            nodes[i][6][64:96] = (gain * (sums[i][0:32] / sums[i][32:33])).astype(bf16)

    for k, (i, h) in enumerate(halves):
        source = nodes[i][2 + h]
        for c in (0, 128):
            nodes[i][5][h, c : c + 128] = matern(scale, dot(source[c : c + 128], targets[i]))
        if k > 0:
            use(*halves[k - 1])
    use(*halves[-1])


def pushed(field, kernel):
    high = jnp.concatenate([field.astype(bf16), jnp.ones((16, field.shape[1]), bf16)], axis=0)
    sums = dot_t(high, kernel)
    return sums[0:32] / sums[32:33]


def sort_in(points, charges, order, source, blocks, rows):
    def fill(b, _):
        lanes = pl.ds(pl.multiple_of(b * 256, 256), 256)
        source[b, 0:64] = points[:, lanes]
        source[b, 64:96] = charges[:, lanes]
        return 0

    lax.fori_loop(0, 16, fill, 0)

    def leaf(g):
        ids = order[:, pl.ds(pl.multiple_of(g * 256, 256), 256)]
        picks = one_hot(ids & 255, 0)
        high = ids >> 8
        stacked = None
        for part in range(SPLIT_IN):
            size = 16 // SPLIT_IN
            found = dot(source[part * size : part * size + size].reshape(size * 96, 256), picks)
            for b in range(size):
                piece = found[b * 96 : b * 96 + 96]
                stacked = piece if stacked is None else jnp.where(high == part * size + b, piece, stacked)
        block = block_of(stacked)
        blocks[OWN + g] = block
        rows[OWN + g] = rows_of(block)

    def some(p, _):
        for q in range(UNROLL_IN):
            leaf(UNROLL_IN * p + q)
        return 0

    lax.fori_loop(0, 16 // UNROLL_IN, some, 0)


SPLIT_IN = 4
UNROLL_IN = 4
UNROLL_OUT = 8
PARTS_OUT = 2
UP_BATCHES = ((0, 1, 2, 3), (4, 5, 6, 7), (8, 9, 10, 11), (12, 13), (14,))


def sort_out(order, fields, output):
    output[...] = jnp.zeros_like(output)

    def some(p, _):
        highs, picks, terms = [], [], []
        for q in range(UNROLL_OUT):
            g = UNROLL_OUT * p + q
            ids = order[:, pl.ds(pl.multiple_of(g * 256, 256), 256)]
            hot = one_hot(ids & 255, 0)
            value = fields[g]
            first = value.astype(bf16)
            second = (value - first.astype(f32)).astype(bf16)
            highs += [ids >> 8]
            picks += [hot, hot]
            terms += [[first, second]]
        picks = jnp.concatenate(picks, axis=1)
        size = 16 // PARTS_OUT
        for part in range(PARTS_OUT):
            masked = []
            for b in range(part * size, part * size + size):
                row = []
                for q in range(UNROLL_OUT):
                    mask = jnp.where(highs[q] == b, 1.0, 0.0).astype(bf16)
                    row += [terms[q][0] * mask, terms[q][1] * mask]
                masked.append(jnp.concatenate(row, axis=1))
            found = dot_t(jnp.concatenate(masked, axis=0), picks)
            for b in range(size):
                lanes = slice((part * size + b) * 256, (part * size + b + 1) * 256)
                output[:, lanes] += found[b * 32 : b * 32 + 32]
        return 0

    lax.fori_loop(0, 16 // UNROLL_OUT, some, 0)


def local_up(scale, skel, blocks, rows, kernels):
    for batch in UP_BATCHES:
        lift_many(
            scale,
            [
                (
                    blocks.at[OWN + 2 * n],
                    blocks.at[OWN + 1 + 2 * n],
                    rows.at[OWN + 2 * n],
                    rows.at[OWN + 1 + 2 * n],
                    skel[n : n + 1, :],
                    kernels.at[n],
                    blocks.at[NODE + n],
                    rows.at[NODE + n],
                )
                for n in batch
            ],
        )


def local_down(fields, kernels):
    for n in range(14, -1, -1):
        field = fields[16 + n]
        fields[2 * n] += pushed(field, kernels[n, 0])
        fields[2 * n + 1] += pushed(field, kernels[n, 1])


def far(scale, far_list, blocks, rows, fields, stage, pairs):
    def count(i, b):
        total = 1.0 if b == i ^ 1 else 0.0
        for e in range(8):
            total = total + jnp.where(far_list[i, e] == b, 1.0, 0.0)
        return total

    def use(i, b, kernel):
        fields[16 + i] += count(i, b) * dot(blocks[NODE + b, 64:96], kernel[...])
        if i != b:
            fields[16 + b] += count(b, i) * dot_t(blocks[NODE + i, 64:96], kernel[...])

    jobs = [
        (
            functools.partial(lambda b: rows[NODE + b], b),
            functools.partial(lambda i: blocks[NODE + i], i),
            functools.partial(use, i, b),
        )
        for i, b in pairs
    ]
    stream(scale, stage, jobs)


def couple(scale, blocks, rows, fields, stage, pairs):
    def use(a, b, kernel):
        fields[16 + b] = dot(blocks[NODE + a, 64:96], kernel[...])
        fields[16 + a] = dot_t(blocks[NODE + b, 64:96], kernel[...])

    jobs = [
        (
            functools.partial(lambda a: rows[NODE + a], a),
            functools.partial(lambda b: blocks[NODE + b], b),
            functools.partial(use, a, b),
        )
        for a, b in pairs
    ]
    stream(scale, stage, jobs)


FAR_PAIRS = [(i, i) for i in range(8)] + [(i, i ^ d) for d in range(1, 8) for i in range(8) if i < i ^ d]


def near_steps(scale, me, near, blocks, rows, fields, stage, g):
    target = blocks[OWN + g]
    total = [jnp.zeros((32, 256), f32)]

    def place(k):
        leaf = near[g, k]
        offset = jnp.clip(leaf - (me - 1) * 16, 0, 47)
        return jnp.where(leaf < 0, ZERO, jnp.where(offset >= 32, offset + 16, offset))

    places = [place(k) for k in range(16)]

    def one(k):
        if k < 16:
            for c in (0, 128):
                stage[k % 2, c : c + 128] = matern(scale, dot(rows[places[k], c : c + 128], target))
        if k > 0:
            total[0] = total[0] + dot(blocks[places[k - 1], 64:96], stage[(k - 1) % 2])
        if k == 16:
            fields[g] = total[0]

    return [functools.partial(one, k) for k in range(17)]


def run(steps, others=(), every=2):
    others = list(others)
    for k, step in enumerate(steps):
        step()
        if others and k % every == 0:
            others.pop(0)()
    for other in others:
        other()


def kernel(
    scale,
    devices,
    points,
    charges,
    order,
    near,
    far_list,
    local_skel,
    upper_skel,
    potentials,
    root,
    blocks,
    rows,
    kernels,
    source,
    fields,
    chain,
    chain_rows,
    chain_kernels,
    chain_fields,
    stage,
    chain_stage,
    side_sent,
    side_got,
    up_sent,
    up_got,
):
    me = lax.axis_index("leaf")
    levels = devices.bit_length() - 1
    after, before = (me + 1) % devices, (me + devices - 1) % devices

    def bit_of(power):
        return (me // power) % 2

    def partner_of(power):
        return me + power * (1 - 2 * bit_of(power))

    barrier = pltpu.get_barrier_semaphore()
    others = [after, before] + [partner_of(2**r) for r in range(levels)]
    for other in others:
        pl.semaphore_signal(barrier, inc=1, device_id=(other,), device_id_type=MESH)
    blocks[ZERO] = jnp.zeros((128, 256), bf16)
    rows[ZERO] = jnp.zeros((256, 128), bf16)
    sort_in(points, charges, order, source, blocks, rows)
    pl.semaphore_wait(barrier, len(others))

    def side_copy(side, target, other):
        return pltpu.make_async_remote_copy(
            src_ref=blocks.at[pl.ds(OWN, 16), 0:96],
            dst_ref=blocks.at[pl.ds(target, 16), 0:96],
            send_sem=side_sent.at[side],
            recv_sem=side_got.at[side],
            device_id=(other,),
            device_id_type=MESH,
        )

    sides = [side_copy(0, LEFT, after), side_copy(1, RIGHT, before)]
    for side in sides:
        side.start()
    local_up(scale, local_skel, blocks, rows, kernels)

    def up_copy(r, power):
        own = bit_of(power)
        return pltpu.make_async_remote_copy(
            src_ref=chain.at[r, own, 0:96],
            dst_ref=chain.at[r, own, 0:96],
            send_sem=up_sent.at[r],
            recv_sem=up_got.at[r],
            device_id=(partner_of(power),),
            device_id_type=MESH,
        )

    def place(r, power, block, flat):
        chain[r, bit_of(power)] = block
        chain_rows[r, bit_of(power)] = flat

    def meet_steps(r, power, last):
        own = bit_of(power)
        kept = {}

        def sibling():
            complete(chain.at[r, 1 - own], chain_rows.at[r, 1 - own])

        def pick():
            row = devices - devices // power + me // (2 * power)
            chosen = upper_skel[pl.ds(row, 1), :]
            picked = dot(chain[r, 0], one_hot(chosen, 0)) + dot(chain[r, 1], one_hot(chosen, 256))
            kept["target"] = picked.astype(bf16)

        def flat():
            chain_rows[r + 1, bit_of(2 * power)] = rows_of(kept["target"])

        def half(h):
            for c in (0, 128):
                piece = matern(scale, dot(chain_rows[r, h, c : c + 128], kept["target"]))
                chain_kernels[r, h, c : c + 128] = piece

        def weigh():
            sums = dot(chain[r, 0, 64:112], chain_kernels[r, 0])
            sums = sums + dot(chain[r, 1, 64:112], chain_kernels[r, 1])
            weights = (gain * (sums[0:32] / sums[32:33])).astype(bf16)
            target = kept["target"]
            chain[r + 1, bit_of(2 * power)] = jnp.concatenate(
                [target[0:64], weights, target[96:128]], axis=0
            )

        def couple_kernel():
            for c in (0, 128):
                chain_stage[c : c + 128] = matern(
                    scale, dot(chain_rows[r, 1 - own, c : c + 128], chain[r, own])
                )

        def couple_use():
            chain_fields[r] = dot(chain[r, 1 - own, 64:96], chain_stage[...])

        if last:
            return [sibling, couple_kernel, couple_use]
        return [
            sibling,
            pick,
            functools.partial(half, 0),
            functools.partial(half, 1),
            couple_kernel,
            weigh,
            flat,
            couple_use,
        ]

    def down(r):
        chain_fields[r] += pushed(chain_fields[r + 1], chain_kernels[r, bit_of(2**r)])

    def leaf(g):
        return near_steps(scale, me, near, blocks, rows, fields, stage, g)

    chain[0, bit_of(1)] = blocks[NODE + 14]
    chain_rows[0, bit_of(1)] = rows[NODE + 14]
    up_copy(0, 1).start()
    def meet(r, power):
        up_copy(r, power).wait()
        run(meet_steps(r, power, False))
        up_copy(r + 1, 2 * power).start()

    fields[16:24] = jnp.zeros((8, 32, 256), f32)
    couple(scale, blocks, rows, fields, stage, [(8, 9), (10, 11), (12, 13)])
    meet(0, 1)
    far(scale, far_list, blocks, rows, fields, stage, FAR_PAIRS)
    meet(1, 2)
    for side in sides:
        side.wait()

    def side_rows(g, _):
        complete(blocks.at[LEFT + g], rows.at[LEFT + g])
        complete(blocks.at[RIGHT + g], rows.at[RIGHT + g])
        return 0

    lax.fori_loop(0, 16, side_rows, 0)

    def some(g, _):
        run(leaf(g))
        return 0

    def step(r, power):
        lo = jnp.where(r < 3, 0, jnp.where(r < 4, 1, jnp.where(r < 5, 3, jnp.where(r < 6, 6, 11))))
        hi = jnp.where(r < 3, 1, jnp.where(r < 4, 3, jnp.where(r < 5, 6, jnp.where(r < 6, 11, 13))))
        lax.fori_loop(lo, hi, some, 0)
        meet(r, power)
        return 2 * power

    lax.fori_loop(2, levels - 1, step, 4)
    lax.fori_loop(13, 15, some, 0)
    up_copy(levels - 1, devices // 2).wait()
    downs = [functools.partial(down, r) for r in range(levels - 2, -1, -1)]
    run(leaf(15), meet_steps(levels - 1, devices // 2, True) + downs, every=1)
    root[0] = chain_fields[0]
    fields[30] = chain_fields[0]
    local_down(fields, kernels)
    potentials[...] = fields[0:16]


def finish(order, fields, root_in, potentials, root):
    root[...] = root_in[...]
    sort_out(order, fields, potentials)


def solution(mesh):
    devices = mesh.shape["leaf"]

    def local(points, charges, order, near, far_list, local_skel, upper_skel):
        vmem = pl.BlockSpec(memory_space=pltpu.VMEM)
        smem = pl.BlockSpec(memory_space=pltpu.SMEM)
        fields, root = pl.pallas_call(
            functools.partial(kernel, 2.0 * math.sqrt(3.0 / 64), devices),
            out_shape=(
                jax.ShapeDtypeStruct((16, 32, 256), f32),
                jax.ShapeDtypeStruct((1, 32, 256), f32),
            ),
            in_specs=[vmem, vmem, vmem, smem, smem, vmem, vmem],
            out_specs=(vmem, vmem),
            scratch_shapes=[
                pltpu.VMEM((64, 128, 256), bf16),
                pltpu.VMEM((64, 256, 128), bf16),
                pltpu.VMEM((15, 2, 256, 256), bf16),
                pltpu.VMEM((16, 96, 256), bf16),
                pltpu.VMEM((31, 32, 256), f32),
                pltpu.VMEM((8, 2, 128, 256), bf16),
                pltpu.VMEM((8, 2, 256, 128), bf16),
                pltpu.VMEM((7, 2, 256, 256), bf16),
                pltpu.VMEM((8, 32, 256), f32),
                pltpu.VMEM((2, 256, 256), bf16),
                pltpu.VMEM((256, 256), bf16),
                pltpu.SemaphoreType.DMA((2,)),
                pltpu.SemaphoreType.DMA((2,)),
                pltpu.SemaphoreType.DMA((8,)),
                pltpu.SemaphoreType.DMA((8,)),
            ],
            compiler_params=pltpu.CompilerParams(
                collective_id=0, has_side_effects=True, vmem_limit_bytes=60 << 20
            ),
            name="tree",
        )(points, charges, order, near, far_list, local_skel, upper_skel)
        return pl.pallas_call(
            finish,
            out_shape=(
                jax.ShapeDtypeStruct((32, 4096), f32),
                jax.ShapeDtypeStruct((1, 32, 256), f32),
            ),
            in_specs=[vmem, vmem, vmem],
            out_specs=(vmem, vmem),
            name="finish",
        )(order, fields, root)

    placed = (
        P(None, "leaf"),
        P(None, "leaf"),
        P("leaf", None),
        P("leaf", None),
        P("leaf", None),
        P("leaf", None),
        P(),
    )
    return jax.shard_map(
        local,
        mesh=mesh,
        in_specs=placed,
        out_specs=(P(None, "leaf"), P("leaf", None, None)),
        check_vma=False,
    )
```
